32 devices in a mesh: gx: 4 (over y, x), gy: 8 (over z, core).
Axes of the slice: x: 2, y: 2, z: 4, core: 2. Of those that a mesh axis runs over, the one named last changes fastest.
Arguments:
- inputs: bfloat16 [512, 8192], P('gx', 'gy'), may hold values from -6 to 6
- out_grad: bfloat16 [512, 8192], P('gx', 'gy'), may hold values from -1.1953125 to 1.1953125
- pre_act: bfloat16 [512, 32768], P('gy', 'gx'), may hold values from -6 to 6
- w_in: bfloat16 [8192, 32768], P('gy', 'gx'), may hold values from -0.0625 to 0.0625
- w_out: bfloat16 [32768, 8192], P('gx', 'gy'), may hold values from -0.03125 to 0.03125
- counts: int32 [4], replicated, may hold values from 1 to 128, 320 in all
Outputs:
- in_grad: bfloat16 [512, 8192], P('gx', 'gy')
- w_in_grad: bfloat16 [8192, 32768], P('gy', 'gx')
- w_out_grad: bfloat16 [32768, 8192], P('gx', 'gy')
The draws below stay inside these ranges and needn't reach their ends.
Inputs may be any that keep to these rules, and one draw needn't show every extreme that they name: In batch shard s (token slots s * 128 to (s + 1) * 128 - 1) the first counts[s] slots are live and the rest are padding; the counts add up to exactly 320, and at least one shard is full.
All inputs are finite; a program needn't handle non-finite values.
Results may differ from the reference program's by a relative error of at most 0.0051.
Values may be sent and summed in bfloat16 or wider, within the bound.
No kernel may reach another device: no remote copies, remote signals or barrier semaphores. Data moves between devices by JAX's collectives and lax.ppermute only.
A program may use at most 192 MiB of HBM per device.

```python
import math
import jax
import jax.numpy as jnp
import numpy as np

D = 8192
FF = 32768
TOK_SHARD = 128
TOKENS = 512
LIVE = 320
N_GX = 4


def shard_levels(own_key, extent, split, least, high):
    loudness = 1.0
    for axis_at, blocks in split:
        draws = jax.random.uniform(jax.random.fold_in(jax.random.fold_in(own_key, 6), axis_at), (blocks,), jnp.float32, least / len(split), high / len(split))
        loudness = loudness * jnp.repeat(jnp.exp(draws), extent[axis_at] // blocks).reshape((-1,) + (1,) * (len(extent) - 1 - axis_at))
    return loudness


def profile(count, total, most, lean):
    portions = [(1 << 20) // math.isqrt(standing ** lean) + 1 for standing in range(2, count + 1)]
    spare, given = total - most - (count - 1), [1] * (count - 1)
    while spare > 0:
        movable = [i for i in range(count - 1) if given[i] < most]
        pool, budget = sum([portions[i] for i in movable]), spare
        for i in movable:
            extra = min(most - given[i], max(1, budget * portions[i] // pool), spare)
            given[i] = given[i] + extra
            spare = spare - extra
    return np.array([most] + given)


def uneven(stream_key, count, total, bound, skew):
    if count == 2:
        one = jax.random.randint(stream_key, (), max(1, total - bound), min(bound, total - 1) + 1)
        return jnp.stack([one, total - one])
    sizes = jnp.asarray(profile(count, total, bound, skew), jnp.int32)
    couples = (count - 1) // 2
    giver, taker = sizes[1:1 + 2 * couples:2], sizes[2:2 + 2 * couples:2]
    margin = jnp.minimum(giver - 1, bound - taker)
    moved = jax.random.randint(jax.random.fold_in(stream_key, 1), (couples,), 0, 1 << 20) % (margin + 1)
    sizes = sizes.at[1:1 + 2 * couples:2].set(giver - moved).at[2:2 + 2 * couples:2].set(taker + moved)
    return sizes[jax.random.permutation(jax.random.fold_in(stream_key, 2), count)]


def gaussian(key, shape, scale, most, shards=(), held_as=jnp.bfloat16):
    result = scale * jax.random.normal(key, shape, jnp.float32)
    if shards:
        result = result * shard_levels(key, shape, shards, -0.22, 0.18)
    return jnp.clip(result, -most, most).astype(held_as)


def setup_inputs(seed: int = 0) -> dict:
    splits = jax.random.split(jax.random.key(seed), 7)
    inputs = gaussian(splits[0], (TOKENS, D), 1.0, 6.0, ((0, 4), (1, 8)))
    out_grad = gaussian(splits[1], (TOKENS, D), 0.2, 1.1953125, ((0, 4), (1, 8)))
    pre_act = gaussian(splits[2], (TOKENS, FF), 1.0, 6.0, ((0, 8), (1, 4)))
    w_in = gaussian(splits[3], (D, FF), D ** -0.5, 0.0625, ((0, 8), (1, 4)))
    w_out = gaussian(splits[4], (FF, D), FF ** -0.5, 0.03125, ((0, 4), (1, 8)))
    counts = uneven(splits[5], N_GX, LIVE, TOK_SHARD, 2).astype(jnp.int32)
    return {"inputs": inputs, "out_grad": out_grad, "pre_act": pre_act, "w_in": w_in, "w_out": w_out, "counts": counts}


gelu_scale = math.sqrt(2.0 / math.pi)
cubic_coef = 0.044715

def gelu_parts(pre):
    inner_arg = gelu_scale * (pre + cubic_coef * pre * pre * pre)
    tangent = jnp.tanh(inner_arg)
    value = 0.5 * pre * (1.0 + tangent)
    slope = 0.5 * (1.0 + tangent) + 0.5 * pre * (1.0 - tangent * tangent) * gelu_scale * (1.0 + 3.0 * cubic_coef * pre * pre)
    return (value, slope)

def reference(inputs, out_grad, pre_act, w_in, w_out, counts):
    positions = jnp.arange(TOKENS, dtype=jnp.int32)
    owner_shard = (positions // TOK_SHARD).astype(jnp.int32)
    is_live = positions % TOK_SHARD < counts[owner_shard]
    masked_grad = jnp.where(is_live[:, None], out_grad, jnp.zeros_like(out_grad))
    value, slope = gelu_parts(pre_act.astype(jnp.float32))
    activation = value.astype(jnp.bfloat16)
    w_out_grad = jnp.dot(activation.T, masked_grad, preferred_element_type=jnp.float32).astype(jnp.bfloat16)
    hidden_sum = jnp.dot(masked_grad, w_out.T, preferred_element_type=jnp.float32)
    hidden_grad = (hidden_sum * slope).astype(jnp.bfloat16)
    w_in_grad = jnp.dot(inputs.T, hidden_grad, preferred_element_type=jnp.float32).astype(jnp.bfloat16)
    in_grad = jnp.dot(hidden_grad, w_in.T, preferred_element_type=jnp.float32).astype(jnp.bfloat16)
    return (in_grad, w_in_grad, w_out_grad)
```

```python
import math

import jax
import jax.numpy as jnp
from jax import lax
from jax.sharding import PartitionSpec as P


CHUNKS = 4
gelu_scale = math.sqrt(2.0 / math.pi)
cubic_coef = 0.044715


def gelu_value(pre):
    tangent = jnp.tanh(gelu_scale * (pre + cubic_coef * pre * pre * pre))
    return 0.5 * pre * (1.0 + tangent)


def gelu_slope(pre):
    tangent = jnp.tanh(gelu_scale * (pre + cubic_coef * pre * pre * pre))
    return 0.5 * (1.0 + tangent) + 0.5 * pre * (1.0 - tangent * tangent) * gelu_scale * (
        1.0 + 3.0 * cubic_coef * pre * pre
    )


def token_sum(left, right):
    return lax.dot_general(
        left, right, (((0,), (0,)), ((), ())), preferred_element_type=jnp.float32
    )


def contract_last(left, right):
    return lax.dot_general(
        left, right, (((1,), (1,)), ((), ())), preferred_element_type=jnp.float32
    )


def pick_rows(slots, table):
    one_hot = slots[:, None] == jnp.arange(table.shape[0], dtype=jnp.int32)[None, :]
    return jnp.dot(
        one_hot.astype(jnp.bfloat16), table, preferred_element_type=jnp.float32
    ).astype(jnp.bfloat16)


def chip_pairs(chips):
    return [(2 * a + c, 2 * b + c) for a, b in chips for c in range(2)]


def body(inputs, out_grad, pre_act, w_in, w_out, counts):
    shards = lax.axis_size("gx")
    chips = lax.axis_size("gy") // 2
    half = chips // 2
    rows = inputs.shape[0]
    lane = pre_act.shape[0]
    width = pre_act.shape[1]
    assert chips == shards and rows == 2 * lane
    live = rows * shards * 5 // 8
    quarter = live // 4
    lane_rows = 2 * quarter
    me_x = lax.axis_index("gx")
    me_y = lax.axis_index("gy")
    chip, core = me_y // 2, me_y % 2
    right = (chip >= half).astype(jnp.int32)
    is_mid = jnp.logical_or(chip == half - 1, chip == half)

    def swap_cores(v):
        return lax.ppermute(v, "gy", [(k, k ^ 1) for k in range(2 * chips)])

    def swap_gx(v, s):
        return lax.ppermute(v, "gx", [(i, i ^ s) for i in range(shards)])

    def send(v, pairs):
        return lax.ppermute(v, "gy", chip_pairs(pairs))

    inward = [[(h, h + 1), (chips - 1 - h, chips - 2 - h)] for h in range(half - 1)]
    across = [(half - 1, half), (half, half - 1)]
    outward = [[(b, a) for a, b in pairs] for pairs in reversed(inward)]

    ends = jnp.cumsum(counts)
    starts = ends - counts
    place = jnp.arange(live, dtype=jnp.int32)
    part = place // quarter
    packed = (
        2 * quarter * jnp.bitwise_xor(part % 2, right)
        + quarter * jnp.bitwise_xor(part // 2, core)
        + place % quarter
    )
    owner = jnp.sum((ends[None, :] <= packed[:, None]).astype(jnp.int32), axis=1)
    owner_hot = owner[:, None] == jnp.arange(shards, dtype=jnp.int32)[None, :]
    inner = packed - jnp.sum(jnp.where(owner_hot, starts[None, :], 0), axis=1)
    gx_slot = jnp.bitwise_xor(owner, me_x) * rows + inner

    dy_all = jnp.concatenate([out_grad] + [swap_gx(out_grad, s) for s in range(1, shards)], axis=0)
    x_all = jnp.concatenate([inputs] + [swap_gx(inputs, s) for s in range(1, shards)], axis=0)
    dy_packed = pick_rows(gx_slot, dy_all)
    x_packed = pick_rows(gx_slot, x_all)

    plus, minus = {0: pre_act}, {0: pre_act}
    for k in range(1, half):
        plus[k] = send(plus[k - 1], [(z, z + 1) for z in range(k - 1, chips - 1)])
        minus[k] = send(minus[k - 1], [(z, z - 1) for z in range(1, chips - k + 1)])
    far = {}
    from_right = send(minus[half - 1], [(z, z - 1) for z in range(1, half + 1)])
    from_left = send(plus[half - 1], [(z, z + 1) for z in range(half - 1, chips - 1)])
    far[half] = jnp.where(right == 1, from_left, from_right)
    for k in range(half + 1, chips):
        far[k] = send(
            far[k - 1],
            [(z, z - 1) for z in range(1, chips - k + 1)]
            + [(z, z + 1) for z in range(k - 1, chips - 1)],
        )

    def both(v):
        return (v, swap_cores(v))

    own = both(pre_act)
    near_plus = {k: both(plus[k]) for k in range(1, half)}
    near_minus = {k: both(minus[k]) for k in range(1, half)}
    far2 = {k: both(far[k]) for k in range(half, chips)}

    near = list(own)
    for k in range(1, half):
        near += list(near_minus[k]) + list(near_plus[k])
    step = owner[:quarter] - chip
    group = jnp.where(step == 0, 0, jnp.where(step > 0, 2 * step - 1, -2 * step))
    lane_of = jnp.bitwise_xor(inner[:quarter] // lane, core)
    near_slot = group * rows + lane_of * lane + inner[:quarter] % lane

    piece = width // CHUNKS
    in_sum = jnp.zeros((live, inputs.shape[1]), jnp.float32)
    w_in_pieces = []
    for f in range(CHUNKS):
        lo, hi = f * piece, (f + 1) * piece
        part_sum = contract_last(dy_packed, w_out[lo:hi])
        got = swap_cores(part_sum[lane_rows:].astype(jnp.bfloat16))
        total = part_sum[:lane_rows] + got.astype(jnp.float32)
        for pairs in inward:
            got = send(total.astype(jnp.bfloat16), pairs)
            total = total + got.astype(jnp.float32)
        got = send(total[quarter:].astype(jnp.bfloat16), across)
        mine = total[:quarter] + got.astype(jnp.float32)
        near_pre = pick_rows(near_slot, jnp.concatenate([v[:, lo:hi] for v in near], axis=0))
        mine = (mine * gelu_slope(near_pre.astype(jnp.float32))).astype(jnp.bfloat16)
        other = send(mine, across)
        for h, pairs in enumerate(outward):
            senders = jnp.logical_or(chip == half - 1 - h, chip == half + h)
            receivers = jnp.logical_or(chip == half - 2 - h, chip == half + 1 + h)
            mine = jnp.where(receivers, send(mine, pairs), mine)
            other = jnp.where(receivers, send(other, pairs), other)
        lane_hidden = jnp.concatenate([mine, other], axis=0)
        hidden_grad = jnp.concatenate([lane_hidden, swap_cores(lane_hidden)], axis=0)
        in_sum = in_sum + contract_last(hidden_grad, w_in[:, lo:hi])
        w_in_pieces.append(token_sum(x_packed, hidden_grad).astype(jnp.bfloat16))
    w_in_grad = jnp.concatenate(w_in_pieces, axis=1)

    slot_row = jnp.arange(rows * shards, dtype=jnp.int32)
    hit = gx_slot[None, :] == slot_row[:, None]
    spread = jnp.dot(
        hit.astype(jnp.bfloat16),
        in_sum.astype(jnp.bfloat16),
        preferred_element_type=jnp.float32,
    ).astype(jnp.bfloat16)
    in_total = spread[:rows].astype(jnp.float32)
    for s in range(1, shards):
        in_total = in_total + swap_gx(spread[s * rows : (s + 1) * rows], s).astype(jnp.float32)

    blocks, shifts = list(own), [0]
    for k in range(1, half):
        ok = chip + k < chips
        blocks += [jnp.where(ok, a, b) for a, b in zip(near_minus[k], far2[chips - k])]
        ok = chip - k >= 0
        blocks += [jnp.where(ok, a, b) for a, b in zip(near_plus[k], far2[chips - k])]
        shifts += [k, chips - k]
    blocks += list(far2[half])
    shifts.append(half)
    pre_all = jnp.concatenate(blocks, axis=0)
    shift_of = jnp.repeat(jnp.array(shifts, jnp.int32), rows)
    token_shard = (chip + shift_of) % chips
    in_block = slot_row % rows
    token_inner = jnp.bitwise_xor(in_block // lane, core) * lane + in_block % lane
    shard_hot = token_shard[:, None] == jnp.arange(shards, dtype=jnp.int32)[None, :]
    is_live = token_inner < jnp.sum(jnp.where(shard_hot, counts[None, :], 0), axis=1)
    dy_slot = jnp.where(is_live, jnp.bitwise_xor(token_shard, me_x) * rows + token_inner, -1)
    dy_ordered = pick_rows(dy_slot, dy_all)
    activation = gelu_value(pre_all.astype(jnp.float32)).astype(jnp.bfloat16)
    w_out_grad = token_sum(activation, dy_ordered)
    return (
        in_total.astype(jnp.bfloat16),
        w_in_grad,
        w_out_grad.astype(jnp.bfloat16),
    )


def solution(mesh):
    return jax.shard_map(
        body,
        mesh=mesh,
        in_specs=(P("gx", "gy"), P("gx", "gy"), P("gy", "gx"), P("gy", "gx"), P("gx", "gy"), P()),
        out_specs=(P("gx", "gy"), P("gy", "gx"), P("gx", "gy")),
        check_vma=False,
    )
```

```python
import math

import jax
import jax.numpy as jnp
from jax import lax
from jax.experimental import pallas as pl
from jax.experimental.pallas import tpu as pltpu
from jax.sharding import PartitionSpec as P


CHUNKS = 4
MATMULS = ((0, 1), (1, 1), (2, 2))
bf16, f32 = jnp.bfloat16, jnp.float32
gelu_scale = math.sqrt(2.0 / math.pi)
cubic_coef = 0.044715


def gelu_value(pre):
    tangent = jnp.tanh(gelu_scale * (pre + cubic_coef * pre * pre * pre))
    return 0.5 * pre * (1.0 + tangent)


def gelu_slope(pre):
    tangent = jnp.tanh(gelu_scale * (pre + cubic_coef * pre * pre * pre))
    return 0.5 * (1.0 + tangent) + 0.5 * pre * (1.0 - tangent * tangent) * gelu_scale * (
        1.0 + 3.0 * cubic_coef * pre * pre
    )


def dot(left, right, over_left, over_right):
    return lax.dot_general(
        left, right, (((over_left,), (over_right,)), ((), ())), preferred_element_type=f32
    )


def cost(flops, bytes_accessed, transcendentals=0):
    return pl.CostEstimate(
        flops=flops, bytes_accessed=bytes_accessed, transcendentals=transcendentals
    )


def one_hot(slots, count):
    return (slots == lax.broadcasted_iota(jnp.int32, (slots.shape[0], count), 1)).astype(bf16)


def column(count):
    return lax.broadcasted_iota(jnp.int32, (count, 1), 0)


class Where:
    def __init__(self, table, rows, shards):
        self.chip, self.core, self.me_x = table[0], table[1], table[2]
        self.counts = [table[3 + s] for s in range(shards)]
        self.rows, self.shards = rows, shards
        self.half_live = rows * shards * 5 // 16

    def owner(self, count):
        place = column(count)
        second = (place >= self.half_live).astype(jnp.int32)
        packed = place - second * self.half_live
        packed = packed + jnp.bitwise_xor(second, self.core) * self.half_live
        owner, inner, end = jnp.zeros_like(packed), packed, 0
        for live in self.counts:
            end = end + live
            past = packed >= end
            owner = owner + past.astype(jnp.int32)
            inner = inner - jnp.where(past, live, 0)
        return owner, inner

    def gx_slot(self):
        owner, inner = self.owner(2 * self.half_live)
        return jnp.bitwise_xor(owner, self.me_x) * self.rows + inner

    def in_lanes(self, inner):
        lane = self.rows // 2
        upper = (inner >= lane).astype(jnp.int32)
        return jnp.bitwise_xor(upper, self.core) * lane + inner - upper * lane

    def pre_slot(self):
        owner, inner = self.owner(self.half_live)
        step = owner - self.chip
        group = jnp.where(step > 0, 2 * step - 1, -2 * step)
        group = jnp.where(jnp.abs(step) == self.shards // 2, self.shards - 1, group)
        return group * self.rows + self.in_lanes(inner)

    def live_count(self, shard):
        total = jnp.zeros_like(shard)
        for s, live in enumerate(self.counts):
            total = jnp.where(shard == s, live, total)
        return total

    def dy_slot(self, shifts):
        slots = []
        for shift in shifts:
            shard = self.chip + shift
            shard = jnp.where(shard >= self.shards, shard - self.shards, shard)
            inner = self.in_lanes(column(self.rows))
            slot = jnp.bitwise_xor(shard, self.me_x) * self.rows + inner
            slots.append(jnp.where(inner < self.live_count(shard), slot, -1))
        return jnp.concatenate(slots, axis=0)

    def unpack_slot(self):
        slots = []
        for s in range(self.shards):
            shard = jnp.bitwise_xor(self.me_x, s)
            begin = 0
            for other, live in enumerate(self.counts):
                begin = begin + jnp.where(other < shard, live, 0)
            inner = column(self.rows)
            packed = begin + inner
            second = (packed >= self.half_live).astype(jnp.int32)
            place = packed - second * self.half_live
            place = place + jnp.bitwise_xor(second, self.core) * self.half_live
            slots.append(jnp.where(inner < self.live_count(shard), place, -1))
        return jnp.concatenate(slots, axis=0)


SMEM = pl.BlockSpec(memory_space=pltpu.SMEM)


def stack(refs):
    return jnp.concatenate([r[...] for r in refs], axis=0)


def pick_rows(table, blocks, shifts):
    rows, model = blocks[0].shape
    shards = len(blocks)
    count = rows * shards
    live = count * 5 // 8

    def kernel(table_ref, *refs):
        where = Where(table_ref, rows, shards)
        packed, ordered = refs[shards:]
        tokens = stack(refs[:shards])
        packed[...] = dot(one_hot(where.gx_slot(), count), tokens, 1, 0).astype(bf16)
        ordered[...] = dot(one_hot(where.dy_slot(shifts), count), tokens, 1, 0).astype(bf16)

    return pl.pallas_call(
        kernel,
        in_specs=[SMEM] + [pl.BlockSpec((rows, model), lambda: (0, 0))] * shards,
        out_shape=[jax.ShapeDtypeStruct((n, model), bf16) for n in (live, count)],
        name="pick_rows",
        cost_estimate=cost(2 * (live + count) * count * model, 2 * (live + 2 * count) * model),
    )(table, *blocks)


def pick_columns(table, blocks):
    rows, model = blocks[0].shape
    shards = len(blocks)
    count = rows * shards
    live = count * 5 // 8

    def kernel(table_ref, *refs):
        hot = one_hot(Where(table_ref, rows, shards).gx_slot(), count)
        refs[-1][...] = dot(stack(refs[:-1]), hot, 0, 1).astype(bf16)

    return pl.pallas_call(
        kernel,
        in_specs=[SMEM] + [pl.BlockSpec((rows, model), lambda: (0, 0))] * shards,
        out_shape=jax.ShapeDtypeStruct((model, live), bf16),
        name="pick_columns",
        cost_estimate=cost(2 * live * count * model, 2 * (live + count) * model),
    )(table, *blocks)


def pick_wide(table, blocks, chunks):
    lane, width = blocks[0].shape
    count = lane * len(blocks)
    picked = count * 5 // 16
    tile = width // chunks

    def kernel(table_ref, *refs):
        ins, outs = refs[: len(blocks)], refs[len(blocks) :]
        hot = one_hot(Where(table_ref, 2 * lane, len(blocks) // 2).pre_slot(), count)
        rows = dot(hot, stack(ins), 1, 0).astype(bf16)
        for k, out in enumerate(outs):

            @pl.when(pl.program_id(0) == k)
            def _():
                out[...] = rows

    return pl.pallas_call(
        kernel,
        grid=(chunks,),
        in_specs=[SMEM] + [pl.BlockSpec((lane, tile), lambda i: (0, i))] * len(blocks),
        out_specs=[pl.BlockSpec((picked, tile), lambda i: (0, 0))] * chunks,
        out_shape=[jax.ShapeDtypeStruct((picked, tile), bf16)] * chunks,
        name="pick_wide",
        cost_estimate=cost(2 * picked * count * width, 2 * width * (picked + count)),
    )(table, *blocks)


def hidden_sums(dy, w_out, first, chunks, wide):
    live, model = dy.shape
    half = live // 2
    split = 2 if chunks == 1 else 1
    tile = wide // split

    def kernel(dy_ref, w_ref, *refs):
        part = dot(dy_ref[...], w_ref[...], 1, 1)
        if chunks == 1:
            refs[0][...] = part[:half]
            refs[1][...] = part[half:].astype(bf16)
            return
        for k in range(chunks):

            @pl.when(pl.program_id(0) == k)
            def _():
                refs[2 * k][...] = part[:half]
                refs[2 * k + 1][...] = part[half:].astype(bf16)

    at = (lambda i: (0, i)) if chunks == 1 else (lambda i: (0, 0))
    outs = pl.pallas_call(
        kernel,
        grid=(chunks * split,),
        in_specs=[
            pl.BlockSpec((live, model), lambda i: (0, 0)),
            pl.BlockSpec((tile, model), lambda i: (first * split + i, 0)),
        ],
        out_specs=[pl.BlockSpec((half, tile), at)] * (2 * chunks),
        out_shape=[jax.ShapeDtypeStruct((half, wide), t) for _ in range(chunks) for t in (f32, bf16)],
        name="hidden_sums",
        cost_estimate=cost(2 * live * model * wide * chunks, 2 * model * wide * chunks),
    )(dy, w_out)
    return list(zip(outs[::2], outs[1::2]))


def in_sum_of(lanes, mates, w_in, first):
    half, wide = lanes[0].shape
    model, chunks = w_in.shape[0], len(lanes)

    def kernel(*refs):
        w_ref, out = refs[2 * chunks :]
        for k in range(chunks):

            @pl.when(pl.program_id(0) == k)
            def _():
                hidden = stack([refs[k], refs[chunks + k]])
                part = dot(hidden, w_ref[...], 1, 1)
                out[...] = part if k == 0 else out[...] + part

    whole = pl.BlockSpec((half, wide), lambda i: (0, 0))
    return pl.pallas_call(
        kernel,
        grid=(chunks,),
        in_specs=[whole] * (2 * chunks) + [pl.BlockSpec((model, wide), lambda i: (0, first + i))],
        out_specs=pl.BlockSpec((2 * half, model), lambda i: (0, 0)),
        out_shape=jax.ShapeDtypeStruct((2 * half, model), f32),
        name="in_sum_of",
        cost_estimate=cost(4 * half * model * wide * chunks, 2 * model * wide * chunks),
    )(*lanes, *mates, w_in)


def in_last(table, lane, mate, w_in, at, before, rows, shards):
    half, wide = lane.shape
    model = w_in.shape[0]
    tile = wide // 2

    def kernel(table_ref, l_ref, m_ref, w_ref, before_ref, *refs):
        outs, acc = refs[:-1], refs[-1]
        part = dot(stack([l_ref, m_ref]), w_ref[...], 1, 1)

        @pl.when(pl.program_id(0) == 0)
        def _():
            acc[...] = before_ref[...] + part

        @pl.when(pl.program_id(0) == 1)
        def _():
            hot = one_hot(Where(table_ref, rows, shards).unpack_slot(), 2 * half)
            spread = dot(hot, (acc[...] + part).astype(bf16), 1, 0).astype(bf16)
            for s, out in enumerate(outs):
                out[...] = spread[s * rows : (s + 1) * rows]

    piece = pl.BlockSpec((half, tile), lambda i: (0, i))
    return pl.pallas_call(
        kernel,
        grid=(2,),
        in_specs=[
            SMEM,
            piece,
            piece,
            pl.BlockSpec((model, tile), lambda i: (0, 2 * at + i)),
            pl.BlockSpec((2 * half, model), lambda i: (0, 0)),
        ],
        out_specs=[pl.BlockSpec((rows, model), lambda i: (0, 0))] * shards,
        out_shape=[jax.ShapeDtypeStruct((rows, model), bf16)] * shards,
        scratch_shapes=[pltpu.VMEM((2 * half, model), f32)],
        name="in_last",
        cost_estimate=cost(4 * half * model * wide, 2 * model * wide + 12 * half * model),
    )(table, lane, mate, w_in, before)


def w_in_grad_of(x_t, lanes, mates):
    half, wide = lanes[0].shape
    model, live = x_t.shape
    chunks = len(lanes)

    def kernel(x_ref, *refs):
        for k in range(chunks):

            @pl.when(pl.program_id(0) == k)
            def _():
                hidden = stack([refs[k], refs[chunks + k]])
                refs[-1][...] = dot(x_ref[...], hidden, 1, 0).astype(bf16)

    whole = pl.BlockSpec((half, wide), lambda i: (0, 0))
    return pl.pallas_call(
        kernel,
        grid=(chunks,),
        in_specs=[pl.BlockSpec((model, live), lambda i: (0, 0))] + [whole] * (2 * chunks),
        out_specs=pl.BlockSpec((model, wide), lambda i: (0, i)),
        out_shape=jax.ShapeDtypeStruct((model, wide * chunks), bf16),
        name="w_in_grad_of",
        cost_estimate=cost(2 * live * model * wide * chunks, 2 * model * wide * chunks),
    )(x_t, *lanes, *mates)


def w_out_grad_of(flags, blocks, spare, dy, grad, first, tiles, tile):
    lane, width = blocks[0].shape
    tokens, model = dy.shape
    places = sorted(spare)

    def kernel(flag_ref, dy_ref, *refs):
        others = dict(zip(places, refs[len(blocks) :]))
        acts = []
        for k in range(len(blocks)):
            pre = refs[k][...].astype(f32)
            if k in others:
                pre = jnp.where(flag_ref[k] == 1, pre, others[k][...].astype(f32))
            acts.append(gelu_value(pre).astype(bf16))
        refs[-1][...] = dot(jnp.concatenate(acts, axis=0), dy_ref[...], 0, 0).astype(bf16)

    block = pl.BlockSpec((lane, tile), lambda i, flag: (0, first + i))
    specs = [pl.BlockSpec((tokens, model), lambda i, flag: (0, 0))]
    specs += [block] * (len(blocks) + len(places))
    operands = [flags, dy, *blocks, *[spare[k] for k in places]]
    aliases = {}
    if grad is not None:
        specs.append(pl.BlockSpec(memory_space=pl.ANY))
        aliases = {len(operands): 0}
        operands.append(grad)
    wide = tiles * tile
    return pl.pallas_call(
        kernel,
        grid_spec=pltpu.PrefetchScalarGridSpec(
            num_scalar_prefetch=1,
            grid=(tiles,),
            in_specs=specs,
            out_specs=pl.BlockSpec((tile, model), lambda i, flag: (first + i, 0)),
        ),
        out_shape=jax.ShapeDtypeStruct((width, model), bf16),
        input_output_aliases=aliases,
        name="w_out_grad_of",
        cost_estimate=cost(
            2 * tokens * model * wide, 2 * wide * (model + tokens), tokens * wide
        ),
    )(*operands)


def chip_pairs(pairs):
    return [(2 * a + c, 2 * b + c) for a, b in pairs for c in range(2)]


def backward(inputs, out_grad, pre_act, w_in, w_out, counts):
    shards = lax.axis_size("gx")
    chips = lax.axis_size("gy") // 2
    half = chips // 2
    rows = inputs.shape[0]
    lane = pre_act.shape[0]
    width = pre_act.shape[1]
    assert chips == shards and rows == 2 * lane
    me_x = lax.axis_index("gx")
    me_y = lax.axis_index("gy")
    chip, core = me_y // 2, me_y % 2

    def swap_cores(v):
        return lax.ppermute(v, "gy", [(k, k ^ 1) for k in range(2 * chips)])

    def swap_gx(v, s):
        return lax.ppermute(v, "gx", [(i, i ^ s) for i in range(shards)])

    def send(v, pairs):
        return lax.ppermute(v, "gy", chip_pairs(pairs))

    inward = [[(h, h + 1), (chips - 1 - h, chips - 2 - h)] for h in range(half - 1)]
    across = [(half - 1, half), (half, half - 1)]
    outward = [[(b, a) for a, b in pairs] for pairs in reversed(inward)]

    dy_blocks = [out_grad] + [swap_gx(out_grad, s) for s in range(1, shards)]
    x_blocks = [inputs] + [swap_gx(inputs, s) for s in range(1, shards)]

    plus, minus = {0: pre_act}, {0: pre_act}
    for k in range(1, half):
        plus[k] = send(plus[k - 1], [(z, z + 1) for z in range(k - 1, chips - 1)])
        minus[k] = send(minus[k - 1], [(z, z - 1) for z in range(1, chips - k + 1)])
    far = {}
    from_right = send(minus[half - 1], [(z, z - 1) for z in range(1, half + 1)])
    from_left = send(plus[half - 1], [(z, z + 1) for z in range(half - 1, chips - 1)])
    far[half] = jnp.where(chip >= half, from_left, from_right)
    for k in range(half + 1, chips):
        far[k] = send(
            far[k - 1],
            [(z, z - 1) for z in range(1, chips - k + 1)]
            + [(z, z + 1) for z in range(k - 1, chips - 1)],
        )

    def both(v):
        return [v, swap_cores(v)]

    blocks, spare, shifts, valid = both(pre_act), {}, [0], [1, 1]
    far2 = {k: both(far[k]) for k in range(half, chips)}
    for k in range(1, half):
        for near, shift, ok in (
            (both(minus[k]), k, chip + k < chips), (both(plus[k]), chips - k, chip >= k)
        ):
            spare[len(blocks)], spare[len(blocks) + 1] = far2[chips - k]
            blocks += near
            shifts.append(shift)
            valid += [ok.astype(jnp.int32)] * 2
    blocks += far2[half]
    shifts.append(half)
    valid += [1, 1]
    flags = jnp.stack([jnp.asarray(v, jnp.int32) for v in valid])

    table = jnp.concatenate([jnp.stack([chip, core, me_x]).astype(jnp.int32), counts])

    dy_packed, dy_ordered = pick_rows(table, dy_blocks, shifts)
    x_t = pick_columns(table, x_blocks)
    pre_packed = pick_wide(table, blocks, CHUNKS)

    wide = width // CHUNKS
    lanes, mates, parts = [], [], []
    for first, count in MATMULS:
        parts += hidden_sums(dy_packed, w_out, first, count, wide)
    for f in range(CHUNKS):
        total, sent = parts[f]
        got = swap_cores(sent)
        total = total + got.astype(f32)
        sent = lax.optimization_barrier(total.astype(bf16))
        for pairs in inward:
            got = send(sent, pairs)
            total = total + got.astype(f32)
            sent = lax.optimization_barrier(total.astype(bf16))
        got = send(sent, across)
        slope = gelu_slope(pre_packed[f].astype(f32))
        hidden = ((total + got.astype(f32)) * slope).astype(bf16)
        hidden = lax.optimization_barrier(hidden)
        for h, pairs in enumerate(outward):
            got = send(hidden, pairs)
            receivers = jnp.logical_or(chip == half - 2 - h, chip == half + 1 + h)
            hidden = jnp.where(receivers, got, hidden)
            hidden = lax.optimization_barrier(hidden)
        lanes.append(hidden)
        mates.append(swap_cores(hidden))

    tile = width // 4
    w_out_grad = w_out_grad_of(flags, blocks, spare, dy_ordered, None, 0, 2, tile)
    w_out_grad = w_out_grad_of(flags, blocks, spare, dy_ordered, w_out_grad, 2, 2, tile)
    in_sum = in_sum_of(lanes[:-1], mates[:-1], w_in, 0)
    spread = in_last(table, lanes[-1], mates[-1], w_in, CHUNKS - 1, in_sum, rows, shards)
    got = [swap_gx(spread[s], s) for s in range(1, shards)]
    w_in_grad = w_in_grad_of(x_t, lanes, mates)
    in_total = spread[0].astype(f32)
    for v in got:
        in_total = in_total + v.astype(f32)
    in_total = in_total.astype(bf16)
    return in_total, w_in_grad, w_out_grad


def solution(mesh):
    return jax.shard_map(
        backward,
        mesh=mesh,
        in_specs=(P("gx", "gy"), P("gx", "gy"), P("gy", "gx"), P("gy", "gx"), P("gx", "gy"), P()),
        out_specs=(P("gx", "gy"), P("gy", "gx"), P("gx", "gy")),
        check_vma=False,
    )
```

```python
import math

import jax
import jax.numpy as jnp
from jax import lax
from jax.experimental import pallas as pl
from jax.experimental.pallas import tpu as pltpu
from jax.sharding import PartitionSpec as P


CHUNKS = 4
MATMULS = ((0, 1), (1, 1), (2, 2))
bf16, f32 = jnp.bfloat16, jnp.float32
gelu_scale = math.sqrt(2.0 / math.pi)
cubic_coef = 0.044715


def gelu_value(pre):
    tangent = jnp.tanh(gelu_scale * (pre + cubic_coef * pre * pre * pre))
    return 0.5 * pre * (1.0 + tangent)


def gelu_slope(pre):
    tangent = jnp.tanh(gelu_scale * (pre + cubic_coef * pre * pre * pre))
    return 0.5 * (1.0 + tangent) + 0.5 * pre * (1.0 - tangent * tangent) * gelu_scale * (
        1.0 + 3.0 * cubic_coef * pre * pre
    )


def dot(left, right, over_left, over_right):
    return lax.dot_general(
        left, right, (((over_left,), (over_right,)), ((), ())), preferred_element_type=f32
    )


def cost(flops, bytes_accessed, transcendentals=0):
    return pl.CostEstimate(
        flops=flops, bytes_accessed=bytes_accessed, transcendentals=transcendentals
    )


def vmem(mib):
    return pltpu.CompilerParams(vmem_limit_bytes=mib << 20)


def one_hot(slots, count):
    return (slots == lax.broadcasted_iota(jnp.int32, (slots.shape[0], count), 1)).astype(bf16)


def column(count):
    return lax.broadcasted_iota(jnp.int32, (count, 1), 0)


class Where:
    def __init__(self, table, rows, shards):
        self.chip, self.core, self.me_x = table[0], table[1], table[2]
        self.counts = [table[3 + s] for s in range(shards)]
        self.rows, self.shards = rows, shards
        self.half_live = rows * shards * 5 // 16

    def owner(self, count):
        place = column(count)
        second = (place >= self.half_live).astype(jnp.int32)
        packed = place - second * self.half_live
        packed = packed + jnp.bitwise_xor(second, self.core) * self.half_live
        owner, inner, end = jnp.zeros_like(packed), packed, 0
        for live in self.counts:
            end = end + live
            past = packed >= end
            owner = owner + past.astype(jnp.int32)
            inner = inner - jnp.where(past, live, 0)
        return owner, inner

    def gx_slot(self):
        owner, inner = self.owner(2 * self.half_live)
        return jnp.bitwise_xor(owner, self.me_x) * self.rows + inner

    def in_lanes(self, inner):
        lane = self.rows // 2
        upper = (inner >= lane).astype(jnp.int32)
        return jnp.bitwise_xor(upper, self.core) * lane + inner - upper * lane

    def pre_slot(self):
        owner, inner = self.owner(self.half_live)
        step = owner - self.chip
        group = jnp.where(step > 0, 2 * step - 1, -2 * step)
        group = jnp.where(jnp.abs(step) == self.shards // 2, self.shards - 1, group)
        return group * self.rows + self.in_lanes(inner)

    def live_count(self, shard):
        total = jnp.zeros_like(shard)
        for s, live in enumerate(self.counts):
            total = jnp.where(shard == s, live, total)
        return total

    def dy_slot(self, shifts):
        slots = []
        for shift in shifts:
            shard = self.chip + shift
            shard = jnp.where(shard >= self.shards, shard - self.shards, shard)
            inner = self.in_lanes(column(self.rows))
            slot = jnp.bitwise_xor(shard, self.me_x) * self.rows + inner
            slots.append(jnp.where(inner < self.live_count(shard), slot, -1))
        return jnp.concatenate(slots, axis=0)

    def unpack_slot(self):
        slots = []
        for s in range(self.shards):
            shard = jnp.bitwise_xor(self.me_x, s)
            begin = 0
            for other, live in enumerate(self.counts):
                begin = begin + jnp.where(other < shard, live, 0)
            inner = column(self.rows)
            packed = begin + inner
            second = (packed >= self.half_live).astype(jnp.int32)
            place = packed - second * self.half_live
            place = place + jnp.bitwise_xor(second, self.core) * self.half_live
            slots.append(jnp.where(inner < self.live_count(shard), place, -1))
        return jnp.concatenate(slots, axis=0)


SMEM = pl.BlockSpec(memory_space=pltpu.SMEM)


def stack(refs):
    return jnp.concatenate([r[...] for r in refs], axis=0)


def pick_rows(table, blocks, shifts):
    rows, model = blocks[0].shape
    shards = len(blocks)
    count = rows * shards
    live = count * 5 // 8

    def kernel(table_ref, *refs):
        where = Where(table_ref, rows, shards)
        packed, ordered = refs[shards:]
        tokens = stack(refs[:shards])
        packed[...] = dot(one_hot(where.gx_slot(), count), tokens, 1, 0).astype(bf16)
        ordered[...] = dot(one_hot(where.dy_slot(shifts), count), tokens, 1, 0).astype(bf16)

    return pl.pallas_call(
        kernel,
        in_specs=[SMEM] + [pl.BlockSpec((rows, model), lambda: (0, 0))] * shards,
        out_shape=[jax.ShapeDtypeStruct((n, model), bf16) for n in (live, count)],
        name="pick_rows",
        compiler_params=vmem(10),
        cost_estimate=cost(2 * (live + count) * count * model, 2 * (live + 2 * count) * model),
    )(table, *blocks)


def pick_columns(table, blocks):
    rows, model = blocks[0].shape
    shards = len(blocks)
    count = rows * shards
    live = count * 5 // 8

    def kernel(table_ref, *refs):
        hot = one_hot(Where(table_ref, rows, shards).gx_slot(), count)
        refs[-1][...] = dot(stack(refs[:-1]), hot, 0, 1).astype(bf16)

    return pl.pallas_call(
        kernel,
        in_specs=[SMEM] + [pl.BlockSpec((rows, model), lambda: (0, 0))] * shards,
        out_shape=jax.ShapeDtypeStruct((model, live), bf16),
        name="pick_columns",
        compiler_params=vmem(8),
        cost_estimate=cost(2 * live * count * model, 2 * (live + count) * model),
    )(table, *blocks)


def pick_wide(table, blocks, chunks):
    lane, width = blocks[0].shape
    count = lane * len(blocks)
    picked = count * 5 // 16
    tile = width // chunks

    def kernel(table_ref, *refs):
        ins, outs = refs[: len(blocks)], refs[len(blocks) :]
        hot = one_hot(Where(table_ref, 2 * lane, len(blocks) // 2).pre_slot(), count)
        rows = dot(hot, stack(ins), 1, 0).astype(bf16)
        for k, out in enumerate(outs):

            @pl.when(pl.program_id(0) == k)
            def _():
                out[...] = rows

    return pl.pallas_call(
        kernel,
        grid=(chunks,),
        in_specs=[SMEM] + [pl.BlockSpec((lane, tile), lambda i: (0, i))] * len(blocks),
        out_specs=[pl.BlockSpec((picked, tile), lambda i: (0, 0))] * chunks,
        out_shape=[jax.ShapeDtypeStruct((picked, tile), bf16)] * chunks,
        name="pick_wide",
        compiler_params=vmem(14),
        cost_estimate=cost(2 * picked * count * width, 2 * width * (picked + count)),
    )(table, *blocks)


def hidden_sums(dy, w_out, first, chunks, wide):
    live, model = dy.shape
    half = live // 2
    split = 2 if chunks == 1 else 1
    tile = wide // split

    def kernel(dy_ref, w_ref, *refs):
        part = dot(dy_ref[...], w_ref[...], 1, 1)
        if chunks == 1:
            refs[0][...] = part[:half]
            refs[1][...] = part[half:].astype(bf16)
            return
        for k in range(chunks):

            @pl.when(pl.program_id(0) == k)
            def _():
                refs[2 * k][...] = part[:half]
                refs[2 * k + 1][...] = part[half:].astype(bf16)

    at = (lambda i: (0, i)) if chunks == 1 else (lambda i: (0, 0))
    outs = pl.pallas_call(
        kernel,
        grid=(chunks * split,),
        in_specs=[
            pl.BlockSpec((live, model), lambda i: (0, 0)),
            pl.BlockSpec((tile, model), lambda i: (first * split + i, 0)),
        ],
        out_specs=[pl.BlockSpec((half, tile), at)] * (2 * chunks),
        out_shape=[jax.ShapeDtypeStruct((half, wide), t) for _ in range(chunks) for t in (f32, bf16)],
        name="hidden_sums",
        compiler_params=vmem(12 if chunks == 1 else 22),
        cost_estimate=cost(2 * live * model * wide * chunks, 2 * model * wide * chunks),
    )(dy, w_out)
    return list(zip(outs[::2], outs[1::2]))


def in_sum_of(lanes, mates, w_in, first):
    half, wide = lanes[0].shape
    model, chunks = w_in.shape[0], len(lanes)

    def kernel(*refs):
        w_ref, out = refs[2 * chunks :]
        for k in range(chunks):

            @pl.when(pl.program_id(0) == k)
            def _():
                hidden = stack([refs[k], refs[chunks + k]])
                part = dot(hidden, w_ref[...], 1, 1)
                out[...] = part if k == 0 else out[...] + part

    whole = pl.BlockSpec((half, wide), lambda i: (0, 0))
    return pl.pallas_call(
        kernel,
        grid=(chunks,),
        in_specs=[whole] * (2 * chunks) + [pl.BlockSpec((model, wide), lambda i: (0, first + i))],
        out_specs=pl.BlockSpec((2 * half, model), lambda i: (0, 0)),
        out_shape=jax.ShapeDtypeStruct((2 * half, model), f32),
        name="in_sum_of",
        compiler_params=vmem(22),
        cost_estimate=cost(4 * half * model * wide * chunks, 2 * model * wide * chunks),
    )(*lanes, *mates, w_in)


def in_last(table, lane, mate, w_in, at, before, rows, shards):
    half, wide = lane.shape
    model = w_in.shape[0]
    tile = wide // 2

    def kernel(table_ref, l_ref, m_ref, w_ref, before_ref, *refs):
        outs, acc = refs[:-1], refs[-1]
        part = dot(stack([l_ref, m_ref]), w_ref[...], 1, 1)

        @pl.when(pl.program_id(0) == 0)
        def _():
            acc[...] = before_ref[...] + part

        @pl.when(pl.program_id(0) == 1)
        def _():
            hot = one_hot(Where(table_ref, rows, shards).unpack_slot(), 2 * half)
            spread = dot(hot, (acc[...] + part).astype(bf16), 1, 0).astype(bf16)
            for s, out in enumerate(outs):
                out[...] = spread[s * rows : (s + 1) * rows]

    piece = pl.BlockSpec((half, tile), lambda i: (0, i))
    return pl.pallas_call(
        kernel,
        grid=(2,),
        in_specs=[
            SMEM,
            piece,
            piece,
            pl.BlockSpec((model, tile), lambda i: (0, 2 * at + i)),
            pl.BlockSpec((2 * half, model), lambda i: (0, 0)),
        ],
        out_specs=[pl.BlockSpec((rows, model), lambda i: (0, 0))] * shards,
        out_shape=[jax.ShapeDtypeStruct((rows, model), bf16)] * shards,
        scratch_shapes=[pltpu.VMEM((2 * half, model), f32)],
        name="in_last",
        compiler_params=vmem(16),
        cost_estimate=cost(4 * half * model * wide, 2 * model * wide + 12 * half * model),
    )(table, lane, mate, w_in, before)


def w_in_grad_of(x_t, lanes, mates):
    half, wide = lanes[0].shape
    model, live = x_t.shape
    chunks = len(lanes)

    def kernel(x_ref, *refs):
        for k in range(chunks):

            @pl.when(pl.program_id(0) == k)
            def _():
                hidden = stack([refs[k], refs[chunks + k]])
                refs[-1][...] = dot(x_ref[...], hidden, 1, 0).astype(bf16)

    whole = pl.BlockSpec((half, wide), lambda i: (0, 0))
    return pl.pallas_call(
        kernel,
        grid=(chunks,),
        in_specs=[pl.BlockSpec((model, live), lambda i: (0, 0))] + [whole] * (2 * chunks),
        out_specs=pl.BlockSpec((model, wide), lambda i: (0, i)),
        out_shape=jax.ShapeDtypeStruct((model, wide * chunks), bf16),
        name="w_in_grad_of",
        compiler_params=vmem(22),
        cost_estimate=cost(2 * live * model * wide * chunks, 2 * model * wide * chunks),
    )(x_t, *lanes, *mates)


def w_out_grad_of(flags, blocks, spare, dy, grad, first, tiles, tile):
    lane, width = blocks[0].shape
    tokens, model = dy.shape
    places = sorted(spare)

    def kernel(flag_ref, dy_ref, *refs):
        others = dict(zip(places, refs[len(blocks) :]))
        acts = []
        for k in range(len(blocks)):
            pre = refs[k][...].astype(f32)
            if k in others:
                pre = jnp.where(flag_ref[k] == 1, pre, others[k][...].astype(f32))
            acts.append(gelu_value(pre).astype(bf16))
        refs[-1][...] = dot(jnp.concatenate(acts, axis=0), dy_ref[...], 0, 0).astype(bf16)

    block = pl.BlockSpec((lane, tile), lambda i, flag: (0, first + i))
    specs = [pl.BlockSpec((tokens, model), lambda i, flag: (0, 0))]
    specs += [block] * (len(blocks) + len(places))
    operands = [flags, dy, *blocks, *[spare[k] for k in places]]
    aliases = {}
    if grad is not None:
        specs.append(pl.BlockSpec(memory_space=pl.ANY))
        aliases = {len(operands): 0}
        operands.append(grad)
    wide = tiles * tile
    return pl.pallas_call(
        kernel,
        grid_spec=pltpu.PrefetchScalarGridSpec(
            num_scalar_prefetch=1,
            grid=(tiles,),
            in_specs=specs,
            out_specs=pl.BlockSpec((tile, model), lambda i, flag: (first + i, 0)),
        ),
        out_shape=jax.ShapeDtypeStruct((width, model), bf16),
        input_output_aliases=aliases,
        name="w_out_grad_of",
        compiler_params=vmem(28),
        cost_estimate=cost(
            2 * tokens * model * wide, 2 * wide * (model + tokens), tokens * wide
        ),
    )(*operands)


def chip_pairs(pairs):
    return [(2 * a + c, 2 * b + c) for a, b in pairs for c in range(2)]


def backward(inputs, out_grad, pre_act, w_in, w_out, counts):
    shards = lax.axis_size("gx")
    chips = lax.axis_size("gy") // 2
    half = chips // 2
    rows = inputs.shape[0]
    lane = pre_act.shape[0]
    width = pre_act.shape[1]
    assert chips == shards and rows == 2 * lane
    me_x = lax.axis_index("gx")
    me_y = lax.axis_index("gy")
    chip, core = me_y // 2, me_y % 2

    def swap_cores(v):
        return lax.ppermute(v, "gy", [(k, k ^ 1) for k in range(2 * chips)])

    def swap_gx(v, s):
        return lax.ppermute(v, "gx", [(i, i ^ s) for i in range(shards)])

    def send(v, pairs):
        return lax.ppermute(v, "gy", chip_pairs(pairs))

    inward = [[(h, h + 1), (chips - 1 - h, chips - 2 - h)] for h in range(half - 1)]
    across = [(half - 1, half), (half, half - 1)]
    outward = [[(b, a) for a, b in pairs] for pairs in reversed(inward)]

    dy_blocks = [out_grad] + [swap_gx(out_grad, s) for s in range(1, shards)]
    x_blocks = [inputs] + [swap_gx(inputs, s) for s in range(1, shards)]

    plus, minus = {0: pre_act}, {0: pre_act}
    for k in range(1, half):
        plus[k] = send(plus[k - 1], [(z, z + 1) for z in range(k - 1, chips - 1)])
        minus[k] = send(minus[k - 1], [(z, z - 1) for z in range(1, chips - k + 1)])
    far = {}
    from_right = send(minus[half - 1], [(z, z - 1) for z in range(1, half + 1)])
    from_left = send(plus[half - 1], [(z, z + 1) for z in range(half - 1, chips - 1)])
    far[half] = jnp.where(chip >= half, from_left, from_right)
    for k in range(half + 1, chips):
        far[k] = send(
            far[k - 1],
            [(z, z - 1) for z in range(1, chips - k + 1)]
            + [(z, z + 1) for z in range(k - 1, chips - 1)],
        )

    def both(v):
        return [v, swap_cores(v)]

    blocks, spare, shifts, valid = both(pre_act), {}, [0], [1, 1]
    far2 = {k: both(far[k]) for k in range(half, chips)}
    for k in range(1, half):
        for near, shift, ok in (
            (both(minus[k]), k, chip + k < chips), (both(plus[k]), chips - k, chip >= k)
        ):
            spare[len(blocks)], spare[len(blocks) + 1] = far2[chips - k]
            blocks += near
            shifts.append(shift)
            valid += [ok.astype(jnp.int32)] * 2
    blocks += far2[half]
    shifts.append(half)
    valid += [1, 1]
    flags = jnp.stack([jnp.asarray(v, jnp.int32) for v in valid])

    table = jnp.concatenate([jnp.stack([chip, core, me_x]).astype(jnp.int32), counts])

    dy_packed, dy_ordered = pick_rows(table, dy_blocks, shifts)
    x_t = pick_columns(table, x_blocks)
    pre_packed = pick_wide(table, blocks, CHUNKS)

    wide = width // CHUNKS
    lanes, mates, parts = [], [], []
    for first, count in MATMULS:
        parts += hidden_sums(dy_packed, w_out, first, count, wide)
    for f in range(CHUNKS):
        total, sent = parts[f]
        got = swap_cores(sent)
        total = total + got.astype(f32)
        sent = lax.optimization_barrier(total.astype(bf16))
        for pairs in inward:
            got = send(sent, pairs)
            total = total + got.astype(f32)
            sent = lax.optimization_barrier(total.astype(bf16))
        got = send(sent, across)
        slope = gelu_slope(pre_packed[f].astype(f32))
        hidden = ((total + got.astype(f32)) * slope).astype(bf16)
        hidden = lax.optimization_barrier(hidden)
        for h, pairs in enumerate(outward):
            got = send(hidden, pairs)
            receivers = jnp.logical_or(chip == half - 2 - h, chip == half + 1 + h)
            hidden = jnp.where(receivers, got, hidden)
            hidden = lax.optimization_barrier(hidden)
        lanes.append(hidden)
        mates.append(swap_cores(hidden))

    tile = width // 8
    w_out_grad = w_out_grad_of(flags, blocks, spare, dy_ordered, None, 0, 4, tile)
    w_out_grad = w_out_grad_of(flags, blocks, spare, dy_ordered, w_out_grad, 4, 4, tile)
    in_sum = in_sum_of(lanes[:-1], mates[:-1], w_in, 0)
    spread = in_last(table, lanes[-1], mates[-1], w_in, CHUNKS - 1, in_sum, rows, shards)
    got = [swap_gx(spread[s], s) for s in range(1, shards)]
    w_in_grad = w_in_grad_of(x_t, lanes, mates)
    in_total = spread[0].astype(f32)
    for v in got:
        in_total = in_total + v.astype(f32)
    in_total = in_total.astype(bf16)
    return in_total, w_in_grad, w_out_grad


def solution(mesh):
    return jax.shard_map(
        backward,
        mesh=mesh,
        in_specs=(P("gx", "gy"), P("gx", "gy"), P("gy", "gx"), P("gy", "gx"), P("gx", "gy"), P()),
        out_specs=(P("gx", "gy"), P("gy", "gx"), P("gx", "gy")),
        check_vma=False,
    )
```

```python
import math

import jax
import jax.numpy as jnp
from jax import lax
from jax.experimental import pallas as pl
from jax.experimental.pallas import tpu as pltpu
from jax.sharding import PartitionSpec as P


CHUNKS = 4
MATMULS = ((0, 1), (1, 1), (2, 2))
bf16, f32 = jnp.bfloat16, jnp.float32
gelu_scale = math.sqrt(2.0 / math.pi)
cubic_coef = 0.044715


def gelu_value(pre):
    tangent = jnp.tanh(gelu_scale * (pre + cubic_coef * pre * pre * pre))
    return 0.5 * pre * (1.0 + tangent)


def gelu_slope(pre):
    tangent = jnp.tanh(gelu_scale * (pre + cubic_coef * pre * pre * pre))
    return 0.5 * (1.0 + tangent) + 0.5 * pre * (1.0 - tangent * tangent) * gelu_scale * (
        1.0 + 3.0 * cubic_coef * pre * pre
    )


def dot(left, right, over_left, over_right):
    return lax.dot_general(
        left, right, (((over_left,), (over_right,)), ((), ())), preferred_element_type=f32
    )


def cost(flops, bytes_accessed, transcendentals=0):
    return pl.CostEstimate(
        flops=flops, bytes_accessed=bytes_accessed, transcendentals=transcendentals
    )


def vmem(mib):
    return pltpu.CompilerParams(vmem_limit_bytes=mib << 20)


def one_hot(slots, count):
    return (slots == lax.broadcasted_iota(jnp.int32, (slots.shape[0], count), 1)).astype(bf16)


def column(count):
    return lax.broadcasted_iota(jnp.int32, (count, 1), 0)


class Where:
    def __init__(self, table, rows, shards):
        self.chip, self.core, self.me_x = table[0], table[1], table[2]
        self.counts = [table[3 + s] for s in range(shards)]
        self.rows, self.shards = rows, shards
        self.half_live = rows * shards * 5 // 16

    def owner(self, count):
        place = column(count)
        second = (place >= self.half_live).astype(jnp.int32)
        packed = place - second * self.half_live
        packed = packed + jnp.bitwise_xor(second, self.core) * self.half_live
        owner, inner, end = jnp.zeros_like(packed), packed, 0
        for live in self.counts:
            end = end + live
            past = packed >= end
            owner = owner + past.astype(jnp.int32)
            inner = inner - jnp.where(past, live, 0)
        return owner, inner

    def gx_slot(self):
        owner, inner = self.owner(2 * self.half_live)
        return jnp.bitwise_xor(owner, self.me_x) * self.rows + inner

    def in_lanes(self, inner):
        lane = self.rows // 2
        upper = (inner >= lane).astype(jnp.int32)
        return jnp.bitwise_xor(upper, self.core) * lane + inner - upper * lane

    def pre_slot(self):
        owner, inner = self.owner(self.half_live)
        step = owner - self.chip
        group = jnp.where(step > 0, 2 * step - 1, -2 * step)
        group = jnp.where(jnp.abs(step) == self.shards // 2, self.shards - 1, group)
        return group * self.rows + self.in_lanes(inner)

    def live_count(self, shard):
        total = jnp.zeros_like(shard)
        for s, live in enumerate(self.counts):
            total = jnp.where(shard == s, live, total)
        return total

    def dy_slot(self, shifts):
        slots = []
        for shift in shifts:
            shard = self.chip + shift
            shard = jnp.where(shard >= self.shards, shard - self.shards, shard)
            inner = self.in_lanes(column(self.rows))
            slot = jnp.bitwise_xor(shard, self.me_x) * self.rows + inner
            slots.append(jnp.where(inner < self.live_count(shard), slot, -1))
        return jnp.concatenate(slots, axis=0)

    def unpack_slot(self):
        slots = []
        for s in range(self.shards):
            shard = jnp.bitwise_xor(self.me_x, s)
            begin = 0
            for other, live in enumerate(self.counts):
                begin = begin + jnp.where(other < shard, live, 0)
            inner = column(self.rows)
            packed = begin + inner
            second = (packed >= self.half_live).astype(jnp.int32)
            place = packed - second * self.half_live
            place = place + jnp.bitwise_xor(second, self.core) * self.half_live
            slots.append(jnp.where(inner < self.live_count(shard), place, -1))
        return jnp.concatenate(slots, axis=0)


SMEM = pl.BlockSpec(memory_space=pltpu.SMEM)


def stack(refs):
    return jnp.concatenate([r[...] for r in refs], axis=0)


def early(table, seconds):
    def kernel(table_ref, out_ref):
        for k in range(table.shape[0]):
            out_ref[k] = table_ref[k]

    return pl.pallas_call(
        kernel,
        in_specs=[SMEM],
        out_specs=SMEM,
        out_shape=jax.ShapeDtypeStruct(table.shape, jnp.int32),
        name="early",
        compiler_params=vmem(1),
        cost_estimate=cost(int(1e15 * seconds), 64),
    )(table)


def pick_rows(table, blocks, shifts):
    rows, model = blocks[0].shape
    shards = len(blocks)
    count = rows * shards
    live = count * 5 // 8

    def kernel(table_ref, *refs):
        where = Where(table_ref, rows, shards)
        packed, ordered = refs[shards:]
        tokens = stack(refs[:shards])
        packed[...] = dot(one_hot(where.gx_slot(), count), tokens, 1, 0).astype(bf16)
        ordered[...] = dot(one_hot(where.dy_slot(shifts), count), tokens, 1, 0).astype(bf16)

    return pl.pallas_call(
        kernel,
        in_specs=[SMEM] + [pl.BlockSpec((rows, model), lambda: (0, 0))] * shards,
        out_shape=[jax.ShapeDtypeStruct((n, model), bf16) for n in (live, count)],
        name="pick_rows",
        compiler_params=vmem(10),
        cost_estimate=cost(2 * (live + count) * count * model, 2 * (live + 2 * count) * model),
    )(table, *blocks)


def pick_columns(table, blocks):
    rows, model = blocks[0].shape
    shards = len(blocks)
    count = rows * shards
    live = count * 5 // 8

    def kernel(table_ref, *refs):
        hot = one_hot(Where(table_ref, rows, shards).gx_slot(), count)
        refs[-1][...] = dot(stack(refs[:-1]), hot, 0, 1).astype(bf16)

    return pl.pallas_call(
        kernel,
        in_specs=[SMEM] + [pl.BlockSpec((rows, model), lambda: (0, 0))] * shards,
        out_shape=jax.ShapeDtypeStruct((model, live), bf16),
        name="pick_columns",
        compiler_params=vmem(8),
        cost_estimate=cost(2 * live * count * model, 2 * (live + count) * model),
    )(table, *blocks)


def pick_wide(table, blocks, chunks):
    lane, width = blocks[0].shape
    count = lane * len(blocks)
    picked = count * 5 // 16
    tile = width // chunks

    def kernel(table_ref, *refs):
        ins, outs = refs[: len(blocks)], refs[len(blocks) :]
        hot = one_hot(Where(table_ref, 2 * lane, len(blocks) // 2).pre_slot(), count)
        rows = dot(hot, stack(ins), 1, 0).astype(bf16)
        for k, out in enumerate(outs):

            @pl.when(pl.program_id(0) == k)
            def _():
                out[...] = rows

    return pl.pallas_call(
        kernel,
        grid=(chunks,),
        in_specs=[SMEM] + [pl.BlockSpec((lane, tile), lambda i: (0, i))] * len(blocks),
        out_specs=[pl.BlockSpec((picked, tile), lambda i: (0, 0))] * chunks,
        out_shape=[jax.ShapeDtypeStruct((picked, tile), bf16)] * chunks,
        name="pick_wide",
        compiler_params=vmem(14),
        cost_estimate=cost(2 * picked * count * width, 2 * width * (picked + count)),
    )(table, *blocks)


def hidden_sums(dy, w_out, first, chunks, wide):
    live, model = dy.shape
    half = live // 2
    split = 2 if chunks == 1 else 1
    tile = wide // split

    def kernel(dy_ref, w_ref, *refs):
        part = dot(dy_ref[...], w_ref[...], 1, 1)
        if chunks == 1:
            refs[0][...] = part[:half]
            refs[1][...] = part[half:].astype(bf16)
            return
        for k in range(chunks):

            @pl.when(pl.program_id(0) == k)
            def _():
                refs[2 * k][...] = part[:half]
                refs[2 * k + 1][...] = part[half:].astype(bf16)

    at = (lambda i: (0, i)) if chunks == 1 else (lambda i: (0, 0))
    outs = pl.pallas_call(
        kernel,
        grid=(chunks * split,),
        in_specs=[
            pl.BlockSpec((live, model), lambda i: (0, 0)),
            pl.BlockSpec((tile, model), lambda i: (first * split + i, 0)),
        ],
        out_specs=[pl.BlockSpec((half, tile), at)] * (2 * chunks),
        out_shape=[jax.ShapeDtypeStruct((half, wide), t) for _ in range(chunks) for t in (f32, bf16)],
        name="hidden_sums",
        compiler_params=vmem(12 if chunks == 1 else 22),
        cost_estimate=cost(2 * live * model * wide * chunks, 2 * model * wide * chunks),
    )(dy, w_out)
    return list(zip(outs[::2], outs[1::2]))


def in_sum_of(lanes, mates, w_in, first):
    half, wide = lanes[0].shape
    model, chunks = w_in.shape[0], len(lanes)

    def kernel(*refs):
        w_ref, out = refs[2 * chunks :]
        for k in range(chunks):

            @pl.when(pl.program_id(0) == k)
            def _():
                hidden = stack([refs[k], refs[chunks + k]])
                part = dot(hidden, w_ref[...], 1, 1)
                out[...] = part if k == 0 else out[...] + part

    whole = pl.BlockSpec((half, wide), lambda i: (0, 0))
    return pl.pallas_call(
        kernel,
        grid=(chunks,),
        in_specs=[whole] * (2 * chunks) + [pl.BlockSpec((model, wide), lambda i: (0, first + i))],
        out_specs=pl.BlockSpec((2 * half, model), lambda i: (0, 0)),
        out_shape=jax.ShapeDtypeStruct((2 * half, model), f32),
        name="in_sum_of",
        compiler_params=vmem(22),
        cost_estimate=cost(4 * half * model * wide * chunks, 2 * model * wide * chunks),
    )(*lanes, *mates, w_in)


def in_last(table, lane, mate, w_in, at, before, rows, shards):
    half, wide = lane.shape
    model = w_in.shape[0]
    tile = wide // 2

    def kernel(table_ref, l_ref, m_ref, w_ref, before_ref, *refs):
        outs, acc = refs[:-1], refs[-1]
        part = dot(stack([l_ref, m_ref]), w_ref[...], 1, 1)

        @pl.when(pl.program_id(0) == 0)
        def _():
            acc[...] = before_ref[...] + part

        @pl.when(pl.program_id(0) == 1)
        def _():
            hot = one_hot(Where(table_ref, rows, shards).unpack_slot(), 2 * half)
            spread = dot(hot, (acc[...] + part).astype(bf16), 1, 0).astype(bf16)
            for s, out in enumerate(outs):
                out[...] = spread[s * rows : (s + 1) * rows]

    piece = pl.BlockSpec((half, tile), lambda i: (0, i))
    return pl.pallas_call(
        kernel,
        grid=(2,),
        in_specs=[
            SMEM,
            piece,
            piece,
            pl.BlockSpec((model, tile), lambda i: (0, 2 * at + i)),
            pl.BlockSpec((2 * half, model), lambda i: (0, 0)),
        ],
        out_specs=[pl.BlockSpec((rows, model), lambda i: (0, 0))] * shards,
        out_shape=[jax.ShapeDtypeStruct((rows, model), bf16)] * shards,
        scratch_shapes=[pltpu.VMEM((2 * half, model), f32)],
        name="in_last",
        compiler_params=vmem(16),
        cost_estimate=cost(4 * half * model * wide, 2 * model * wide + 12 * half * model),
    )(table, lane, mate, w_in, before)


def w_in_grad_of(x_t, lanes, mates):
    half, wide = lanes[0].shape
    model, live = x_t.shape
    chunks = len(lanes)

    def kernel(x_ref, *refs):
        for k in range(chunks):

            @pl.when(pl.program_id(0) == k)
            def _():
                hidden = stack([refs[k], refs[chunks + k]])
                refs[-1][...] = dot(x_ref[...], hidden, 1, 0).astype(bf16)

    whole = pl.BlockSpec((half, wide), lambda i: (0, 0))
    return pl.pallas_call(
        kernel,
        grid=(chunks,),
        in_specs=[pl.BlockSpec((model, live), lambda i: (0, 0))] + [whole] * (2 * chunks),
        out_specs=pl.BlockSpec((model, wide), lambda i: (0, i)),
        out_shape=jax.ShapeDtypeStruct((model, wide * chunks), bf16),
        name="w_in_grad_of",
        compiler_params=vmem(22),
        cost_estimate=cost(2 * live * model * wide * chunks, 2 * model * wide * chunks),
    )(x_t, *lanes, *mates)


def w_out_grad_of(flags, blocks, spare, dy, grad, first, tiles, tile):
    lane, width = blocks[0].shape
    tokens, model = dy.shape
    places = sorted(spare)

    def kernel(flag_ref, dy_ref, *refs):
        others = dict(zip(places, refs[len(blocks) :]))
        acts = []
        for k in range(len(blocks)):
            pre = refs[k][...].astype(f32)
            if k in others:
                pre = jnp.where(flag_ref[k] == 1, pre, others[k][...].astype(f32))
            acts.append(gelu_value(pre).astype(bf16))
        refs[-1][...] = dot(jnp.concatenate(acts, axis=0), dy_ref[...], 0, 0).astype(bf16)

    block = pl.BlockSpec((lane, tile), lambda i, flag: (0, first + i))
    specs = [pl.BlockSpec((tokens, model), lambda i, flag: (0, 0))]
    specs += [block] * (len(blocks) + len(places))
    operands = [flags, dy, *blocks, *[spare[k] for k in places]]
    aliases = {}
    if grad is not None:
        specs.append(pl.BlockSpec(memory_space=pl.ANY))
        aliases = {len(operands): 0}
        operands.append(grad)
    wide = tiles * tile
    return pl.pallas_call(
        kernel,
        grid_spec=pltpu.PrefetchScalarGridSpec(
            num_scalar_prefetch=1,
            grid=(tiles,),
            in_specs=specs,
            out_specs=pl.BlockSpec((tile, model), lambda i, flag: (first + i, 0)),
        ),
        out_shape=jax.ShapeDtypeStruct((width, model), bf16),
        input_output_aliases=aliases,
        name="w_out_grad_of",
        compiler_params=vmem(28),
        cost_estimate=cost(
            2 * tokens * model * wide, 2 * wide * (model + tokens), tokens * wide
        ),
    )(*operands)


def chip_pairs(pairs):
    return [(2 * a + c, 2 * b + c) for a, b in pairs for c in range(2)]


def backward(inputs, out_grad, pre_act, w_in, w_out, counts):
    shards = lax.axis_size("gx")
    chips = lax.axis_size("gy") // 2
    half = chips // 2
    rows = inputs.shape[0]
    lane = pre_act.shape[0]
    width = pre_act.shape[1]
    assert chips == shards and rows == 2 * lane
    me_x = lax.axis_index("gx")
    me_y = lax.axis_index("gy")
    chip, core = me_y // 2, me_y % 2

    def swap_cores(v):
        return lax.ppermute(v, "gy", [(k, k ^ 1) for k in range(2 * chips)])

    def swap_gx(v, s):
        return lax.ppermute(v, "gx", [(i, i ^ s) for i in range(shards)])

    def send(v, pairs):
        return lax.ppermute(v, "gy", chip_pairs(pairs))

    inward = [[(h, h + 1), (chips - 1 - h, chips - 2 - h)] for h in range(half - 1)]
    across = [(half - 1, half), (half, half - 1)]
    outward = [[(b, a) for a, b in pairs] for pairs in reversed(inward)]

    dy_blocks = [out_grad] + [swap_gx(out_grad, s) for s in range(1, shards)]
    x_blocks = [inputs] + [swap_gx(inputs, s) for s in range(1, shards)]

    plus, minus = {0: pre_act}, {0: pre_act}
    for k in range(1, half):
        plus[k] = send(plus[k - 1], [(z, z + 1) for z in range(k - 1, chips - 1)])
        minus[k] = send(minus[k - 1], [(z, z - 1) for z in range(1, chips - k + 1)])
    far = {}
    from_right = send(minus[half - 1], [(z, z - 1) for z in range(1, half + 1)])
    from_left = send(plus[half - 1], [(z, z + 1) for z in range(half - 1, chips - 1)])
    far[half] = jnp.where(chip >= half, from_left, from_right)
    for k in range(half + 1, chips):
        far[k] = send(
            far[k - 1],
            [(z, z - 1) for z in range(1, chips - k + 1)]
            + [(z, z + 1) for z in range(k - 1, chips - 1)],
        )

    def both(v):
        return [v, swap_cores(v)]

    blocks, spare, shifts, valid = both(pre_act), {}, [0], [1, 1]
    far2 = {k: both(far[k]) for k in range(half, chips)}
    for k in range(1, half):
        for near, shift, ok in (
            (both(minus[k]), k, chip + k < chips), (both(plus[k]), chips - k, chip >= k)
        ):
            spare[len(blocks)], spare[len(blocks) + 1] = far2[chips - k]
            blocks += near
            shifts.append(shift)
            valid += [ok.astype(jnp.int32)] * 2
    blocks += far2[half]
    shifts.append(half)
    valid += [1, 1]
    flags = jnp.stack([jnp.asarray(v, jnp.int32) for v in valid])

    table = jnp.concatenate([jnp.stack([chip, core, me_x]).astype(jnp.int32), counts])

    table = early(table, 25e-6)
    dy_packed, dy_ordered = pick_rows(table, dy_blocks, shifts)
    x_t = pick_columns(table, x_blocks)
    pre_packed = pick_wide(table, blocks, CHUNKS)

    wide = width // CHUNKS
    lanes, mates, parts = [], [], []
    for first, count in MATMULS:
        parts += hidden_sums(dy_packed, w_out, first, count, wide)
    for f in range(CHUNKS):
        total, sent = parts[f]
        got = swap_cores(sent)
        total = total + got.astype(f32)
        sent = lax.optimization_barrier(total.astype(bf16))
        for pairs in inward:
            got = send(sent, pairs)
            total = total + got.astype(f32)
            sent = lax.optimization_barrier(total.astype(bf16))
        got = send(sent, across)
        slope = gelu_slope(pre_packed[f].astype(f32))
        hidden = ((total + got.astype(f32)) * slope).astype(bf16)
        hidden = lax.optimization_barrier(hidden)
        for h, pairs in enumerate(outward):
            got = send(hidden, pairs)
            receivers = jnp.logical_or(chip == half - 2 - h, chip == half + 1 + h)
            hidden = jnp.where(receivers, got, hidden)
            hidden = lax.optimization_barrier(hidden)
        lanes.append(hidden)
        mates.append(swap_cores(hidden))

    tile = width // 8
    w_out_grad = w_out_grad_of(flags, blocks, spare, dy_ordered, None, 0, 4, tile)
    w_out_grad = w_out_grad_of(flags, blocks, spare, dy_ordered, w_out_grad, 4, 4, tile)
    in_sum = in_sum_of(lanes[:-1], mates[:-1], w_in, 0)
    spread = in_last(table, lanes[-1], mates[-1], w_in, CHUNKS - 1, in_sum, rows, shards)
    got = [swap_gx(spread[s], s) for s in range(1, shards)]
    w_in_grad = w_in_grad_of(x_t, lanes, mates)
    in_total = spread[0].astype(f32)
    for v in got:
        in_total = in_total + v.astype(f32)
    in_total = in_total.astype(bf16)
    return in_total, w_in_grad, w_out_grad


def solution(mesh):
    return jax.shard_map(
        backward,
        mesh=mesh,
        in_specs=(P("gx", "gy"), P("gx", "gy"), P("gy", "gx"), P("gy", "gx"), P("gx", "gy"), P()),
        out_specs=(P("gx", "gy"), P("gy", "gx"), P("gx", "gy")),
        check_vma=False,
    )
```
